128 devices in a mesh: dp: 4 (over x_lo, core), ctx: 32 (over x_hi, y, z).
Axes of the slice: x: 4 (x_hi: 2, x_lo: 2; x = x_hi * 2 + x_lo), y: 4, z: 4, core: 2. Of those that a mesh axis runs over, the one named last changes fastest.
Arguments:
- frames: bfloat16 [4, 160, 16, 16, 512], P('dp', 'ctx'), may hold values from -6 to 6
- stream: bfloat16 [4, 160, 64, 3072], P('dp', 'ctx'), may hold values from -6 to 6
- video_frames: int32 [4], P('dp'), may hold values from 1 to 160
- conv_weight: bfloat16 [3, 3, 3, 512, 512], replicated, may hold values from -0.0546875 to 0.0546875
- latent_weight: bfloat16 [512, 16], replicated, may hold values from -0.25 to 0.25
- embed_weight: bfloat16 [64, 3072], replicated, may hold values from -0.75 to 0.75
- norm_gain: float32 [3072], replicated, may hold values from 0.25 to 1.75
- qkv_weight: bfloat16 [3072, 4608], P('ctx', 'dp'), may hold values from -0.109375 to 0.109375
Outputs:
- section: bfloat16 [4, 160, 16, 16, 512], P('dp', 'ctx')
- mixed: bfloat16 [4, 160, 64, 1536], P('dp', 'ctx')
The draws below stay inside these ranges and needn't reach their ends.
All inputs are finite; a program needn't handle non-finite values.
Results may differ from the reference program's by a relative error of at most 0.0061.
Values may be sent and summed in bfloat16 or wider, within the bound.
A program may use at most 128 MiB of HBM per device.

```python
import jax
import jax.numpy as jnp
from jax import lax

CH = 512
LAT = 16
D = 3072
HEADS = 12
HD = 128
HT = 16
WT = 16
NF = 160
GROUPS = 4
TOKF = 64


def with_ends(entries, rng, least, largest):
    shape = entries.shape
    spot = [jax.random.randint(jax.random.fold_in(rng, axis), (), 0, shape[axis]) for axis in range(len(shape))]
    entries = entries.at[tuple(spot)].set(least)
    longest = shape.index(max(shape))
    spot[longest] = (spot[longest] + 1) % shape[longest]
    return entries.at[tuple(spot)].set(largest)


def block_scale(rng, extent, pieces, low, top_value):
    def one(position, blocks):
        heights = jax.random.uniform(jax.random.fold_in(jax.random.fold_in(rng, 6), position), (blocks,), jnp.float32, low / len(pieces), top_value / len(pieces))
        return jnp.repeat(jnp.exp(heights), extent[position] // blocks).reshape((-1,) + (1,) * (len(extent) - position - 1))

    gain = one(*pieces[0])
    for cut in pieces[1:]:
        gain = gain * one(*cut)
    return gain


def gaussian(own_key, dims, deviation, most, cuts=(), held_as=jnp.bfloat16):
    factor_of = block_scale(own_key, dims, cuts, -0.22, 0.18) if cuts else 1.0
    values = jax.random.normal(own_key, dims, jnp.float32) * deviation * factor_of
    return jnp.minimum(jnp.maximum(values, -most), most).astype(held_as)


def setup_inputs(seed: int = 0) -> dict:
    seeds = jax.random.split(jax.random.key(seed), 9)
    frames = gaussian(seeds[0], (GROUPS, NF, HT, WT, CH), 1.0, 6.0, ((0, 4), (1, 32)))
    stream = gaussian(seeds[1], (GROUPS, NF, TOKF, D), 1.0, 6.0, ((0, 4), (1, 32)))
    video_frames = with_ends(jax.random.randint(seeds[2], (GROUPS,), 1, NF + 1), jax.random.fold_in(seeds[2], 1), 1, NF).astype(jnp.int32)
    conv_weight = gaussian(seeds[3], (3, 3, 3, CH, CH), (27 * CH) ** -0.5, 0.0546875)
    latent_weight = gaussian(seeds[4], (CH, LAT), CH ** -0.5, 0.25)
    embed_weight = gaussian(seeds[5], (4 * LAT, D), (4 * LAT) ** -0.5, 0.75)
    norm_gain = jnp.clip(1.0 + 0.15 * jax.random.normal(seeds[6], (D,), jnp.float32), 0.25, 1.75)
    qkv_weight = gaussian(seeds[7], (D, 3 * HEADS * HD), D ** -0.5, 0.109375, ((0, 32), (1, 4)))
    return dict(frames=frames, stream=stream, video_frames=video_frames, conv_weight=conv_weight, latent_weight=latent_weight, embed_weight=embed_weight, norm_gain=norm_gain, qkv_weight=qkv_weight)


def conv_group(args):
    act_group, length, conv_weight = args
    padded = jnp.pad(act_group, ((2, 0), (1, 1), (1, 1), (0, 0)))
    frame_ids = jnp.arange(NF, dtype=jnp.int32)
    total = jnp.zeros((NF * HT * WT, CH), jnp.float32)
    for lag in range(3):
        part = jnp.zeros((NF * HT * WT, CH), jnp.float32)
        for row in range(3):
            for col in range(3):
                slab = padded[2 - lag:2 - lag + NF, row:row + HT, col:col + WT, :].reshape(-1, CH)
                part = part + jnp.dot(slab, conv_weight[lag, row, col], preferred_element_type=jnp.float32)
        if lag == 0:
            total = total + part
        else:
            valid = ((frame_ids < length) & (frame_ids >= lag)).astype(jnp.float32)
            total = total + part * jnp.repeat(valid, HT * WT)[:, None]
    return total

def attend_group(args):
    block, length = args
    query = block[..., 0:HD].astype(jnp.float32)
    keys = block[..., HD:2 * HD].astype(jnp.float32)
    values = block[..., 2 * HD:3 * HD].astype(jnp.float32)
    scores = jnp.einsum('tphd,sphd->phts', query, keys, precision=lax.Precision.HIGHEST) * HD ** (-0.5)
    frame_ids = jnp.arange(NF, dtype=jnp.int32)
    video = frame_ids < length
    allowed = video[:, None] & video[None, :] | (frame_ids[:, None] == frame_ids[None, :])
    scores = jnp.where(allowed, scores, -1e+30)
    top = lax.optimization_barrier(jnp.max(scores, axis=-1, keepdims=True))
    expo = jnp.exp(scores - top)
    probs = (expo / lax.optimization_barrier(jnp.sum(expo, axis=-1, keepdims=True))).astype(jnp.bfloat16)
    out = jnp.einsum('phts,sphd->tphd', probs.astype(jnp.float32), values, precision=lax.Precision.HIGHEST)
    return out.astype(jnp.bfloat16)

def reference(frames, stream, video_frames, conv_weight, latent_weight, embed_weight, norm_gain, qkv_weight):
    act = jax.nn.silu(frames.astype(jnp.float32)).astype(jnp.bfloat16)
    conv = lax.map(lambda pair: conv_group((pair[0], pair[1], conv_weight)), (act, video_frames))
    section = (frames.astype(jnp.float32) + conv.reshape(frames.shape)).astype(jnp.bfloat16)
    latent = jnp.dot(section.reshape(-1, CH), latent_weight, preferred_element_type=jnp.float32).astype(jnp.bfloat16)
    latent = latent.reshape(GROUPS, NF, HT // 2, 2, WT // 2, 2, LAT).transpose(0, 1, 2, 4, 3, 5, 6)
    patches = latent.reshape(-1, 4 * LAT)
    embedded = jnp.dot(patches, embed_weight, preferred_element_type=jnp.float32) + stream.reshape(-1, D).astype(jnp.float32)
    scale = lax.rsqrt(lax.optimization_barrier(jnp.mean(embedded * embedded, axis=-1, keepdims=True)) + 1e-06)
    normed = (embedded * scale * norm_gain).astype(jnp.bfloat16)
    qkv = jnp.dot(normed, qkv_weight, preferred_element_type=jnp.float32).astype(jnp.bfloat16)
    qkv = qkv.reshape(GROUPS, NF, TOKF, HEADS, 3 * HD)
    mixed = lax.map(attend_group, (qkv, video_frames))
    return (section, mixed.reshape(GROUPS, NF, TOKF, HEADS * HD))
```

```python
import functools

import jax
import jax.numpy as jnp
from jax import lax
from jax.experimental import pallas as pl
from jax.experimental.pallas import tpu as pltpu
from jax.sharding import Mesh
from jax.sharding import PartitionSpec as P

AXES = ("xl", "co", "xh", "y", "z")
CTX = ("xh", "y", "z")
MESH = pl.DeviceIdType.MESH
F32 = jnp.float32
BF16 = jnp.bfloat16
NCTX = 32
LANES = 128


def place():
    return {a: lax.axis_index(a) for a in AXES}


def ctx_of(me):
    return (me["xh"] * 4 + me["y"]) * 4 + me["z"]


def at_ctx(me, c, co=None):
    return (me["xl"], me["co"] if co is None else co, c // 16, (c // 4) % 4, c % 4)


def coordinate(me, axis):
    return (me["xh"] * 2 + me["xl"], me["y"], me["z"])[axis]


def moved(me, axis, c):
    if axis == 0:
        return (c % 2, me["co"], c // 2, me["y"], me["z"])
    if axis == 1:
        return (me["xl"], me["co"], me["xh"], c, me["z"])
    return (me["xl"], me["co"], me["xh"], me["y"], c)


def gather_copies(me, wall, ssem, rsem):
    rows = wall.shape[4] // 3
    half = rows // 2
    stages = [[] for _ in range(6)]
    for part in range(3):
        for phase in range(3):
            axis = (part + phase) % 3
            full = [(part + i) % 3 for i in range(phase)]
            c = coordinate(me, axis)
            for step in range(2):
                for way in range(2):
                    sign = 1 - 2 * way
                    to = (c + sign + 4) % 4
                    held = c if step == 0 else (c - sign + 4) % 4
                    begin = part * rows + (half if step and way else 0)
                    size = half if step else rows
                    index = []
                    for a in range(3):
                        if a in full:
                            got = None
                        elif a == axis:
                            got = held
                        else:
                            got = coordinate(me, a)
                        if a == 0:
                            if got is None:
                                index += [pl.ds(0, 2), pl.ds(0, 2)]
                            else:
                                index += [got % 2, got // 2]
                        else:
                            index.append(pl.ds(0, 4) if got is None else got)
                    block = wall.at[(*index, pl.ds(begin, size))]
                    n = ((part * 3 + phase) * 2 + step) * 2 + way
                    stages[phase * 2 + step].append(
                        pltpu.make_async_remote_copy(
                            src_ref=block,
                            dst_ref=block,
                            send_sem=ssem.at[n],
                            recv_sem=rsem.at[n],
                            device_id=moved(me, axis, to),
                            device_id_type=MESH,
                        )
                    )
    return stages


def section_kernel(
    frames, stream, length, cw, lw4, ew, gain, w,
    sec_out, wall, xr,
    xin, xcat, cwv, acc, secb, strm, nt, sb, sent,
    cw_sem, in_sem, w_ssem, w_rsem, h_ssem, h_rsem, a_ssem, a_rsem, out_sem, own_sem,
):
    me = place()
    ctx = ctx_of(me)
    mine = wall.at[me["xl"], me["xh"], me["y"], me["z"]]
    place_w = pltpu.make_async_copy(w, mine, own_sem.at[0])
    place_w.start()
    load_frames = pltpu.make_async_copy(frames, xin.at[pl.ds(2, 5)], in_sem.at[0])
    load_frames.start()

    def load_cw(s):
        return pltpu.make_async_copy(cw.at[s], cwv.at[s], cw_sem.at[s])

    def order(k):
        return (2 - k // 3) * 3 + k % 3

    for k in range(9):
        load_cw(order(k)).start()
    load_stream = pltpu.make_async_copy(stream, strm, in_sem.at[1])
    load_stream.start()

    barrier = pltpu.get_barrier_semaphore()

    @pl.loop(1, NCTX)
    def _(k):
        pl.semaphore_signal(
            barrier, inc=1, device_id=at_ctx(me, (ctx + k) % NCTX), device_id_type=MESH
        )

    x = coordinate(me, 0)
    for d in (1, 3):
        pl.semaphore_signal(
            barrier, inc=1, device_id=moved(me, 0, (x + d) % 4), device_id_type=MESH
        )
    pl.semaphore_wait(barrier, NCTX + 1)

    halo = pltpu.make_async_remote_copy(
        src_ref=frames.at[pl.ds(3, 2)],
        dst_ref=xin.at[pl.ds(0, 2)],
        send_sem=h_ssem,
        recv_sem=h_rsem,
        device_id=at_ctx(me, (ctx + 1) % NCTX),
        device_id_type=MESH,
    )
    halo.start()
    place_w.wait()
    stages = gather_copies(me, wall, w_ssem, w_rsem)

    def start_stage(k):
        if k:
            for copy in stages[k - 1]:
                copy.wait_recv()
        for copy in stages[k]:
            copy.start()

    start_stage(0)

    edge = jnp.zeros((7, 1, 16, 1536), BF16)
    xcat[:, pl.ds(0, 1)] = edge
    xcat[:, pl.ds(17, 1)] = edge
    column = lax.broadcasted_iota(jnp.int32, (256, 512), 0) & 15

    def spread(i, factor):
        v = xin[i].astype(F32)
        act = (v / (1.0 + jnp.exp(-v))).astype(BF16).astype(F32) * factor
        before = jnp.where(column == 0, 0.0, pltpu.roll(act, 1, 0))
        after = jnp.where(column == 15, 0.0, pltpu.roll(act, 255, 0))
        for b, part in enumerate((before, act, after)):
            xcat[i, pl.ds(1, 16), :, pl.ds(512 * b, 512)] = part.astype(BF16).reshape(16, 16, 512)

    load_frames.wait()

    @pl.loop(2, 7)
    def _(i):
        spread(i, 1.0)

    cell = lax.broadcasted_iota(jnp.int32, (256, 64), 0)
    lane = lax.broadcasted_iota(jnp.int32, (256, 64), 1)
    corner = ((cell >> 4) & 1) * 2 + (cell & 1)
    keep = jnp.where((lane >> 4) == corner, 1.0, 0.0)
    tok = lax.broadcasted_iota(jnp.int32, (64, 256), 0)
    cel = lax.broadcasted_iota(jnp.int32, (64, 256), 1)
    pick = jnp.where((cel >> 5) * 8 + ((cel & 15) >> 1) == tok, 1.0, 0.0).astype(BF16)
    count = length[0]

    def conv(first, many, checkpoints, arrive):
        acc[pl.ds(0, many * 256)] = jnp.zeros((many * 256, 512), F32)

        @pl.loop(0, 9)
        def _(k):
            if arrive:
                load_cw(order(k)).wait()
            for when, stage in checkpoints:
                @pl.when(k == when)
                def _():
                    start_stage(stage)

            @pl.when(k == 6)
            def _():
                for f in range(many):
                    video = jnp.where(ctx * 5 + first + f < count, 1.0, 0.0)
                    acc[pl.ds(f * 256, 256)] = acc[pl.ds(f * 256, 256)] * video

            lag = 2 - k // 3
            slab = xcat[pl.ds(first + 2 - lag, many), pl.ds(k % 3, 16)]
            acc[pl.ds(0, many * 256)] += jnp.dot(
                slab.reshape(many * 256, 1536), cwv[order(k)], preferred_element_type=F32
            )

    def finish(first, many, n):
        @pl.loop(0, many)
        def _(i):
            t = first + i
            sec = (xin[t + 2].astype(F32) + acc[pl.ds(pl.multiple_of(i * 256, 256), 256)]).astype(BF16)
            secb[t] = sec
            lat = jnp.dot(sec, lw4[...], preferred_element_type=F32).astype(BF16).astype(F32)
            patches = jnp.dot(pick, (lat * keep).astype(BF16), preferred_element_type=F32).astype(BF16)
            e = jnp.dot(patches, ew[...], preferred_element_type=F32) + strm[t].astype(F32)
            scale = lax.rsqrt(jnp.mean(e * e, axis=-1, keepdims=True) + 1e-06)
            e = e * scale * gain[...]
            for j in range(24):
                nt[pl.ds(j, 64, stride=24), :] = e[:, j * LANES : (j + 1) * LANES]
            sb[t] = nt[...].astype(BF16).reshape(32, 48, LANES)

        span = pl.ds(first, many)
        pltpu.make_async_copy(secb.at[span], sec_out.at[span], out_sem.at[n]).start()
        stage = pltpu.make_async_copy(sb.at[span], sent.at[span], own_sem.at[1 + n])
        stage.start()
        stage.wait()

        @pl.loop(1, NCTX)
        def _(k):
            to = (ctx + k) % NCTX
            pltpu.make_async_remote_copy(
                src_ref=sent.at[span, to],
                dst_ref=xr.at[ctx, span],
                send_sem=a_ssem.at[n],
                recv_sem=a_rsem.at[n],
                device_id=at_ctx(me, to),
                device_id_type=MESH,
            ).start()

        pltpu.make_async_copy(sent.at[span, ctx], xr.at[ctx, span], own_sem.at[3 + n]).start()

    conv(2, 3, ((2, 1), (5, 2)), True)
    start_stage(3)
    load_stream.wait()
    finish(2, 3, 0)
    halo.wait_recv()
    inner = jnp.where(ctx > 0, 1.0, 0.0)

    @pl.loop(0, 2)
    def _(i):
        spread(i, inner)

    conv(0, 2, ((3, 4),), False)
    finish(0, 2, 1)
    start_stage(5)
    for copy in stages[5]:
        copy.wait_recv()
    for stage in stages:
        for copy in stage:
            copy.wait_send()
    halo.wait_send()
    for n, (first, many) in enumerate(((2, 3), (0, 2))):
        span = pl.ds(first, many)
        bulk = xr.at[pl.ds(0, NCTX - 1), span]
        pltpu.make_async_copy(bulk, bulk, a_rsem.at[n]).wait()
        pltpu.make_async_copy(bulk, bulk, a_ssem.at[n]).wait()
        pltpu.make_async_copy(sent.at[span, ctx], xr.at[ctx, span], own_sem.at[3 + n]).wait()
        pltpu.make_async_copy(secb.at[span], sec_out.at[span], out_sem.at[n]).wait()


def sections(frames, stream, length, cw, lw4, ew, gain, w):
    hbm = pl.BlockSpec(memory_space=pl.ANY)
    vmem = pl.BlockSpec(memory_space=pltpu.VMEM)
    smem = pl.BlockSpec(memory_space=pltpu.SMEM)
    dma = pltpu.SemaphoreType.DMA
    return pl.pallas_call(
        section_kernel,
        out_shape=(
            jax.ShapeDtypeStruct((5, 256, 512), BF16),
            jax.ShapeDtypeStruct((2, 2, 4, 4, 96, 1152), BF16),
            jax.ShapeDtypeStruct((NCTX, 5, 48, LANES), BF16),
        ),
        in_specs=[hbm, hbm, smem, hbm, vmem, vmem, vmem, vmem],
        out_specs=(hbm, hbm, hbm),
        scratch_shapes=[
            pltpu.VMEM((7, 256, 512), BF16),
            pltpu.VMEM((7, 18, 16, 1536), BF16),
            pltpu.VMEM((9, 1536, 512), BF16),
            pltpu.VMEM((768, 512), F32),
            pltpu.VMEM((5, 256, 512), BF16),
            pltpu.VMEM((5, 64, 3072), BF16),
            pltpu.VMEM((1536, LANES), F32),
            pltpu.VMEM((5, 32, 48, LANES), BF16),
            pltpu.VMEM((5, 32, 48, LANES), BF16),
            dma((9,)), dma((2,)), dma((36,)), dma((36,)), dma, dma, dma((2,)), dma((2,)), dma((2,)), dma((5,)),
        ],
        compiler_params=pltpu.CompilerParams(
            collective_id=0, has_side_effects=True, vmem_limit_bytes=60 * 2**20
        ),
        name="sections",
    )(frames, stream, length, cw, lw4, ew, gain, w)


def attention_kernel(
    wall, xr, lens, out,
    wv, xs, lsib, xf, xm, qs, of, osd, sent, orr, off, outf,
    w_sem, x_ssem, x_rsem, o_ssem, o_rsem, own_sem,
):
    me = place()
    ctx = ctx_of(me)
    co = me["co"]

    def load_w(h):
        return pltpu.make_async_copy(
            wall.at[h // 3, :, pl.ds(pl.multiple_of((h % 3) * 384, 128), 384)], wv.at[h], w_sem.at[h]
        )

    for h in range(6):
        load_w(h).start()

    barrier = pltpu.get_barrier_semaphore()

    @pl.loop(1, NCTX)
    def _(k):
        pl.semaphore_signal(
            barrier, inc=1, device_id=at_ctx(me, (ctx + k) % NCTX), device_id_type=MESH
        )

    @pl.loop(0, NCTX)
    def _(k):
        pl.semaphore_signal(
            barrier, inc=1, device_id=at_ctx(me, (ctx + k) % NCTX, 1 - co), device_id_type=MESH
        )

    pl.semaphore_wait(barrier, 2 * NCTX - 1)
    swaps = [
        pltpu.make_async_remote_copy(
            src_ref=a,
            dst_ref=b,
            send_sem=x_ssem.at[n],
            recv_sem=x_rsem.at[n],
            device_id=at_ctx(me, ctx, 1 - co),
            device_id_type=MESH,
        )
        for n, (a, b) in enumerate(((xr, xs), (lens, lsib)))
    ]
    for copy in swaps:
        copy.start()

    row = lax.broadcasted_iota(jnp.int32, (160, 160), 0)
    col = lax.broadcasted_iota(jnp.int32, (160, 160), 1)
    row_frame = (row & 31) * 5 + (row >> 5)
    col_frame = (col & 31) * 5 + (col >> 5)
    same = row == col

    for g in range(2):
        if g:
            for copy in swaps:
                copy.wait_recv()
        src, lref = ((xr, lens), (xs, lsib))[g]
        xf[...] = src[...].astype(F32)
        for f in range(5):
            for pos in range(2):
                for j in range(24):
                    xm[pl.ds(pos * 160 + f * 32, 32), pl.ds(j * LANES, LANES)] = xf[
                        pl.ds((f * 2 + pos) * 24 + j, 32, stride=240), :
                    ].astype(BF16)
        most = jnp.broadcast_to(lref[0:1, 0:1], (160, 160))
        allowed = ((row_frame < most) & (col_frame < most)) | same

        @pl.loop(0, 6)
        def _(h):
            if g == 0:
                load_w(h).wait()
            qs[...] = jnp.dot(xm[...], wv[h], preferred_element_type=F32).astype(BF16)
            for pos in range(2):
                rows = pl.ds(pos * 160, 160)
                scores = lax.dot_general(
                    qs[rows, 0:128], qs[rows, 128:256], (((1,), (1,)), ((), ())),
                    preferred_element_type=F32,
                ) * (128.0 ** -0.5)
                scores = jnp.where(allowed, scores, -1e30)
                expo = jnp.exp(scores - jnp.max(scores, axis=-1, keepdims=True))
                probs = (expo / jnp.sum(expo, axis=-1, keepdims=True)).astype(BF16)
                o = jnp.dot(probs, qs[rows, 256:384], preferred_element_type=F32)
                for f in range(5):
                    of[pl.ds(f * 12 + pos * 6 + h, 32, stride=64), :] = o[f * 32 : (f + 1) * 32]

        osd[g] = of[...].astype(BF16).reshape(NCTX, 64, LANES)
        stage = pltpu.make_async_copy(osd.at[g], sent.at[g], own_sem.at[g])
        stage.start()
        stage.wait()

        @pl.loop(1 - g, NCTX)
        def _(k):
            to = (ctx + k) % NCTX
            pltpu.make_async_remote_copy(
                src_ref=sent.at[g, to],
                dst_ref=orr.at[co, ctx],
                send_sem=o_ssem.at[g],
                recv_sem=o_rsem.at[g],
                device_id=at_ctx(me, to, co if g == 0 else 1 - co),
                device_id_type=MESH,
            ).start()

        if g == 0:
            pltpu.make_async_copy(sent.at[0, ctx], orr.at[co, ctx], own_sem.at[2]).start()

    pltpu.make_async_copy(sent.at[0, ctx], orr.at[co, ctx], own_sem.at[2]).wait()
    for copy in swaps:
        copy.wait_send()
    for g in range(2):
        bulk = orr.at[0, pl.ds(0, NCTX - 1 + g)]
        pltpu.make_async_copy(bulk, bulk, o_rsem.at[g]).wait()
        pltpu.make_async_copy(bulk, bulk, o_ssem.at[g]).wait()
    off[...] = orr[...].astype(F32).reshape(2 * NCTX * 64, LANES)
    for c in range(2):
        for h in range(6):
            head = 6 * (h // 3) + 3 * c + h % 3
            for f in range(5):
                for pos in range(2):
                    outf[pl.ds(head * 320 + f * 64 + pos, 32, stride=2), :] = off[
                        pl.ds(c * 2048 + f * 12 + pos * 6 + h, 32, stride=64), :
                    ]
    for head in range(12):
        out[:, pl.ds(head * LANES, LANES)] = outf[pl.ds(head * 320, 320)].astype(BF16)


def attention(wall, xr, lens):
    hbm = pl.BlockSpec(memory_space=pl.ANY)
    vmem = pl.BlockSpec(memory_space=pltpu.VMEM)
    dma = pltpu.SemaphoreType.DMA
    return pl.pallas_call(
        attention_kernel,
        out_shape=jax.ShapeDtypeStruct((320, 1536), BF16),
        in_specs=[hbm, vmem, vmem],
        out_specs=vmem,
        scratch_shapes=[
            pltpu.VMEM((6, 3072, 384), BF16),
            pltpu.VMEM((7680, LANES), BF16),
            pltpu.VMEM((8, LANES), jnp.int32),
            pltpu.VMEM((7680, LANES), F32),
            pltpu.VMEM((320, 3072), BF16),
            pltpu.VMEM((320, 384), BF16),
            pltpu.VMEM((2048, LANES), F32),
            pltpu.VMEM((2, NCTX, 64, LANES), BF16),
            pltpu.VMEM((2, NCTX, 64, LANES), BF16),
            pltpu.VMEM((2, NCTX, 64, LANES), BF16),
            pltpu.VMEM((4096, LANES), F32),
            pltpu.VMEM((3840, LANES), F32),
            dma((6,)), dma((2,)), dma((2,)), dma((2,)), dma((2,)), dma((3,)),
        ],
        compiler_params=pltpu.CompilerParams(
            collective_id=1, has_side_effects=True, vmem_limit_bytes=60 * 2**20
        ),
        name="attention",
    )(wall, xr, lens)


def on_device(frames, stream, video_frames, conv_weight, latent_weight, embed_weight, norm_gain, qkv_weight):
    section, wall, xr = sections(
        frames.reshape(5, 256, 512),
        stream.reshape(5, 64, 3072),
        video_frames,
        conv_weight.reshape(9, 1536, 512),
        jnp.tile(latent_weight, (1, 4)),
        embed_weight,
        norm_gain.reshape(1, 3072),
        qkv_weight,
    )
    lens = jnp.broadcast_to(video_frames[0], (8, LANES))
    mixed = attention(wall.reshape(2, 3072, 1152), xr.reshape(7680, LANES), lens)
    return section.reshape(frames.shape), mixed.reshape(1, 5, 64, 1536)


def solution(mesh):
    finer = Mesh(mesh.devices.reshape(2, 2, 2, 4, 4), AXES)
    dp = ("xl", "co")
    return jax.shard_map(
        on_device,
        mesh=finer,
        in_specs=(
            P(dp, CTX, None, None, None),
            P(dp, CTX, None, None),
            P(dp),
            P(),
            P(),
            P(),
            P(),
            P(CTX, dp),
        ),
        out_specs=(P(dp, CTX, None, None, None), P(dp, CTX, None, None)),
        check_vma=False,
    )
```

```python
import jax
import jax.numpy as jnp
from jax import lax
from jax.experimental import pallas as pl
from jax.experimental.pallas import tpu as pltpu
from jax.sharding import Mesh
from jax.sharding import PartitionSpec as P

AXES = ("xl", "co", "xh", "y", "z")
CTX = ("xh", "y", "z")
MESH = pl.DeviceIdType.MESH
F32 = jnp.float32
BF16 = jnp.bfloat16
NCTX = 32
LANES = 128


def place():
    return {a: lax.axis_index(a) for a in AXES}


def ctx_of(me):
    return (me["xh"] * 4 + me["y"]) * 4 + me["z"]


def at_ctx(me, c, co=None):
    return (me["xl"], me["co"] if co is None else co, c // 16, (c // 4) % 4, c % 4)


def coordinate(me, axis):
    return (me["xh"] * 2 + me["xl"], me["y"], me["z"])[axis]


def moved(me, axis, c):
    if axis == 0:
        return (c % 2, me["co"], c // 2, me["y"], me["z"])
    if axis == 1:
        return (me["xl"], me["co"], me["xh"], c, me["z"])
    return (me["xl"], me["co"], me["xh"], me["y"], c)


def gather_copies(me, wall, ssem, rsem, r):
    rows = wall.shape[5] // 3
    half = rows // 2
    stages = [[] for _ in range(6)]
    for part in range(3):
        for phase in range(3):
            axis = (part + phase) % 3
            full = [(part + i) % 3 for i in range(phase)]
            c = coordinate(me, axis)
            for step in range(2):
                for way in range(2):
                    sign = 1 - 2 * way
                    to = (c + sign + 4) % 4
                    held = c if step == 0 else (c - sign + 4) % 4
                    begin = part * rows + (half if step and way else 0)
                    size = half if step else rows
                    index = [r]
                    for a in range(3):
                        if a in full:
                            got = None
                        elif a == axis:
                            got = held
                        else:
                            got = coordinate(me, a)
                        if a == 0:
                            if got is None:
                                index += [pl.ds(0, 2), pl.ds(0, 2)]
                            else:
                                index += [got % 2, got // 2]
                        else:
                            index.append(pl.ds(0, 4) if got is None else got)
                    block = wall.at[(*index, pl.ds(begin, size))]
                    n = (((r * 3 + part) * 3 + phase) * 2 + step) * 2 + way
                    stages[phase * 2 + step].append(
                        pltpu.make_async_remote_copy(
                            src_ref=block,
                            dst_ref=block,
                            send_sem=ssem.at[n],
                            recv_sem=rsem.at[n],
                            device_id=moved(me, axis, to),
                            device_id_type=MESH,
                        )
                    )
    return stages


TICKS = (
    ((0, 0),),
    ((0, 1),),
    ((0, 2), (1, 0)),
    ((0, 3), (1, 1)),
    ((0, 4), (1, 2)),
    ((0, 5), (1, 3), (2, 0)),
    ((1, 4), (2, 1)),
    ((1, 5), (2, 2)),
    ((2, 3),),
    ((2, 4),),
    ((2, 5),),
)


def block_kernel(
    frames, stream, length, lens, cw, lw4, ew, gain, w,
    sec_out, out,
    xin, xcat, cwv, acc, secb, strm, nt, sb, sent, wall, xr, xs, lboth, xf, xm, qs, of, osd, osent, orr,
    cw_sem, in_sem, w_ssem, w_rsem, h_ssem, h_rsem, a_ssem, a_rsem, out_sem, own_sem,
    x_ssem, x_rsem, o_ssem, o_rsem, o_own,
):
    me = place()
    ctx = ctx_of(me)
    co = me["co"]
    place_w = [
        pltpu.make_async_copy(
            w.at[:, pl.ds(384 * r, 384)],
            wall.at[r, me["xl"], me["xh"], me["y"], me["z"]],
            own_sem.at[5 + r],
        )
        for r in range(3)
    ]
    for copy in place_w:
        copy.start()
    load_frames = pltpu.make_async_copy(frames, xin.at[pl.ds(2, 5)], in_sem.at[0])
    load_frames.start()

    def order(n):
        k = n % 9
        return (2 - k // 3) * 3 + k % 3

    def load_cw(n):
        return pltpu.make_async_copy(cw.at[order(n)], cwv.at[n % 4], cw_sem.at[n % 4])

    for n in range(3):
        load_cw(n).start()
    load_stream = pltpu.make_async_copy(stream, strm, in_sem.at[1])
    load_stream.start()

    barrier = pltpu.get_barrier_semaphore()

    @pl.loop(1, NCTX)
    def _(k):
        pl.semaphore_signal(
            barrier, inc=1, device_id=at_ctx(me, (ctx + k) % NCTX), device_id_type=MESH
        )

    @pl.loop(0, NCTX)
    def _(k):
        pl.semaphore_signal(
            barrier, inc=1, device_id=at_ctx(me, (ctx + k) % NCTX, 1 - co), device_id_type=MESH
        )

    x = coordinate(me, 0)
    for d in (1, 3):
        pl.semaphore_signal(
            barrier, inc=1, device_id=moved(me, 0, (x + d) % 4), device_id_type=MESH
        )
    pl.semaphore_wait(barrier, 2 * NCTX + 1)

    halo = pltpu.make_async_remote_copy(
        src_ref=frames.at[pl.ds(3, 2)],
        dst_ref=xin.at[pl.ds(0, 2)],
        send_sem=h_ssem,
        recv_sem=h_rsem,
        device_id=at_ctx(me, (ctx + 1) % NCTX),
        device_id_type=MESH,
    )
    halo.start()
    for copy in place_w:
        copy.wait()
    rounds = [gather_copies(me, wall, w_ssem, w_rsem, r) for r in range(3)]

    def tick(n):
        for r, stage in TICKS[n]:
            if stage:
                for copy in rounds[r][stage - 1]:
                    copy.wait_recv()
            for copy in rounds[r][stage]:
                copy.start()

    tick(0)

    edge = jnp.zeros((7, 1, 16, 1536), BF16)
    xcat[:, pl.ds(0, 1)] = edge
    xcat[:, pl.ds(17, 1)] = edge
    column = lax.broadcasted_iota(jnp.int32, (256, 512), 0) & 15

    def spread(i, factor):
        v = xin[i].astype(F32)
        act = (v / (1.0 + jnp.exp(-v))).astype(BF16).astype(F32) * factor
        before = jnp.where(column == 0, 0.0, pltpu.roll(act, 1, 0))
        after = jnp.where(column == 15, 0.0, pltpu.roll(act, 255, 0))
        for b, part in enumerate((before, act, after)):
            xcat[i, pl.ds(1, 16), :, pl.ds(512 * b, 512)] = part.astype(BF16).reshape(16, 16, 512)

    load_frames.wait()

    @pl.loop(2, 7)
    def _(i):
        spread(i, 1.0)

    tick(1)
    cell = lax.broadcasted_iota(jnp.int32, (256, 64), 0)
    lane = lax.broadcasted_iota(jnp.int32, (256, 64), 1)
    corner = ((cell >> 4) & 1) * 2 + (cell & 1)
    keep = jnp.where((lane >> 4) == corner, 1.0, 0.0)
    tok = lax.broadcasted_iota(jnp.int32, (64, 256), 0)
    cel = lax.broadcasted_iota(jnp.int32, (64, 256), 1)
    pick = jnp.where((cel >> 5) * 8 + ((cel & 15) >> 1) == tok, 1.0, 0.0).astype(BF16)
    count = length[0]

    def conv(first, many, checkpoints, begin):
        acc[pl.ds(0, many * 256)] = jnp.zeros((many * 256, 512), F32)

        @pl.loop(0, 9)
        def _(k):
            n = begin + k
            load_cw(n).wait()

            @pl.when(n < 15)
            def _():
                load_cw(n + 3).start()

            for when, now in checkpoints:
                @pl.when(k == when)
                def _():
                    tick(now)

            @pl.when(k == 6)
            def _():
                for f in range(many):
                    video = jnp.where(ctx * 5 + first + f < count, 1.0, 0.0)
                    acc[pl.ds(f * 256, 256)] = acc[pl.ds(f * 256, 256)] * video

            lag = 2 - k // 3
            slab = xcat[pl.ds(first + 2 - lag, many), pl.ds(k % 3, 16)]
            acc[pl.ds(0, many * 256)] += jnp.dot(
                slab.reshape(many * 256, 1536), cwv[n % 4], preferred_element_type=F32
            )

    def finish(first, many, n):
        @pl.loop(0, many)
        def _(i):
            t = first + i
            sec = (xin[t + 2].astype(F32) + acc[pl.ds(pl.multiple_of(i * 256, 256), 256)]).astype(BF16)
            secb[t] = sec
            lat = jnp.dot(sec, lw4[...], preferred_element_type=F32).astype(BF16).astype(F32)
            patches = jnp.dot(pick, (lat * keep).astype(BF16), preferred_element_type=F32).astype(BF16)
            e = jnp.dot(patches, ew[...], preferred_element_type=F32) + strm[t].astype(F32)
            scale = lax.rsqrt(jnp.mean(e * e, axis=-1, keepdims=True) + 1e-06)
            e = e * scale * gain[...]
            for j in range(24):
                nt[pl.ds(j, 64, stride=24), :] = e[:, j * LANES : (j + 1) * LANES]
            sb[t] = nt[...].astype(BF16).reshape(32, 48, LANES)

        span = pl.ds(first, many)
        pltpu.make_async_copy(secb.at[span], sec_out.at[span], out_sem.at[n]).start()
        stage = pltpu.make_async_copy(sb.at[span], sent.at[span], own_sem.at[1 + n])
        stage.start()
        stage.wait()

        @pl.loop(1, NCTX)
        def _(k):
            to = (ctx + k) % NCTX
            pltpu.make_async_remote_copy(
                src_ref=sent.at[span, to],
                dst_ref=xr.at[ctx, span],
                send_sem=a_ssem.at[n],
                recv_sem=a_rsem.at[n],
                device_id=at_ctx(me, to),
                device_id_type=MESH,
            ).start()

        pltpu.make_async_copy(sent.at[span, ctx], xr.at[ctx, span], own_sem.at[3 + n]).start()

    conv(2, 3, ((1, 2), (4, 3), (8, 4)), 0)
    load_stream.wait()
    finish(2, 3, 0)
    tick(5)
    halo.wait_recv()
    inner = jnp.where(ctx > 0, 1.0, 0.0)

    @pl.loop(0, 2)
    def _(i):
        spread(i, inner)

    conv(0, 2, ((5, 6),), 9)
    finish(0, 2, 1)
    tick(7)

    for n, (first, many) in enumerate(((2, 3), (0, 2))):
        span = pl.ds(first, many)
        bulk = xr.at[pl.ds(0, NCTX - 1), span]
        pltpu.make_async_copy(bulk, bulk, a_rsem.at[n]).wait()
        pltpu.make_async_copy(sent.at[span, ctx], xr.at[ctx, span], own_sem.at[3 + n]).wait()
    swaps = [
        pltpu.make_async_remote_copy(
            src_ref=a,
            dst_ref=b,
            send_sem=x_ssem.at[n],
            recv_sem=x_rsem.at[n],
            device_id=at_ctx(me, ctx, 1 - co),
            device_id_type=MESH,
        )
        for n, (a, b) in enumerate(((xr, xs), (lens, lboth.at[1])))
    ]
    for copy in swaps:
        copy.start()
    tick(8)
    lboth[0] = lens[...]

    def fill(g, src):
        xf[...] = src[...].astype(F32).reshape(7680, LANES)
        for f in range(5):
            for pos in range(2):
                for j in range(24):
                    xm[g, pl.ds(pos * 160 + f * 32, 32), pl.ds(j * LANES, LANES)] = xf[
                        pl.ds((f * 2 + pos) * 24 + j, 32, stride=240), :
                    ].astype(BF16)

    fill(0, xr)
    tick(9)
    for copy in swaps:
        copy.wait_recv()
    fill(1, xs)
    for copy in rounds[0][5]:
        copy.wait_recv()

    row = lax.broadcasted_iota(jnp.int32, (160, 160), 0)
    col = lax.broadcasted_iota(jnp.int32, (160, 160), 1)
    row_frame = (row & 31) * 5 + (row >> 5)
    col_frame = (col & 31) * 5 + (col >> 5)
    same = row == col

    def returned(r, g, to):
        return pltpu.make_async_remote_copy(
            src_ref=osent.at[r, g, to],
            dst_ref=orr.at[r, co, ctx],
            send_sem=o_ssem.at[r * 2 + g],
            recv_sem=o_rsem.at[r * 2 + g],
            device_id=at_ctx(me, to, co if g == 0 else 1 - co),
            device_id_type=MESH,
        )

    def kept(r):
        return pltpu.make_async_copy(osent.at[r, 0, ctx], orr.at[r, co, ctx], o_own.at[r])

    @pl.loop(0, 3)
    def _(r):
        @pl.when(r == 1)
        def _():
            tick(10)
            for copy in rounds[1][5]:
                copy.wait_recv()

        @pl.when(r == 2)
        def _():
            for copy in rounds[2][5]:
                copy.wait_recv()

        @pl.loop(0, 4)
        def _(q):
            g = q // 2
            hq = q % 2
            qs[...] = jnp.dot(
                xm[g], wall[r, hq].reshape(3072, 384), preferred_element_type=F32
            ).astype(BF16)
            most = jnp.broadcast_to(lboth[g, 0:1, 0:1], (160, 160))
            allowed = ((row_frame < most) & (col_frame < most)) | same
            for pos in range(2):
                rows = pl.ds(pos * 160, 160)
                scores = lax.dot_general(
                    qs[rows, 0:128], qs[rows, 128:256], (((1,), (1,)), ((), ())),
                    preferred_element_type=F32,
                ) * (128.0 ** -0.5)
                scores = jnp.where(allowed, scores, -1e30)
                expo = jnp.exp(scores - jnp.max(scores, axis=-1, keepdims=True))
                probs = (expo / jnp.sum(expo, axis=-1, keepdims=True)).astype(BF16)
                o = jnp.dot(probs, qs[rows, 256:384], preferred_element_type=F32)
                for f in range(5):
                    of[pl.ds(g * 768 + f * 4 + pos * 2 + hq, 32, stride=24), :] = o[
                        f * 32 : (f + 1) * 32
                    ]

        osd[r] = of[...].astype(BF16).reshape(2, NCTX, 24, LANES)
        stage = pltpu.make_async_copy(osd.at[r], osent.at[r], own_sem.at[0])
        stage.start()
        stage.wait()

        @pl.loop(1, NCTX)
        def _(k):
            returned(r, 0, (ctx + k) % NCTX).start()

        @pl.loop(0, NCTX)
        def _(k):
            returned(r, 1, (ctx + k) % NCTX).start()

        kept(r).start()

    for stages in rounds:
        for stage in stages:
            for copy in stage:
                copy.wait_send()
    halo.wait_send()
    for copy in swaps:
        copy.wait_send()
    for n, (first, many) in enumerate(((2, 3), (0, 2))):
        span = pl.ds(first, many)
        bulk = xr.at[pl.ds(0, NCTX - 1), span]
        pltpu.make_async_copy(bulk, bulk, a_ssem.at[n]).wait()
        pltpu.make_async_copy(secb.at[span], sec_out.at[span], out_sem.at[n]).wait()
    for r in range(3):
        kept(r).wait()
        for g in range(2):
            bulk = orr.at[0, 0, pl.ds(0, NCTX - 1 + g)]
            pltpu.make_async_copy(bulk, bulk, o_rsem.at[r * 2 + g]).wait()
            pltpu.make_async_copy(bulk, bulk, o_ssem.at[r * 2 + g]).wait()
    xf[pl.ds(0, 4608)] = orr[...].astype(F32).reshape(4608, LANES)
    for r in range(3):
        for c in range(2):
            for hq in range(2):
                head = 6 * hq + 3 * c + r
                for f in range(5):
                    for pos in range(2):
                        xf[pl.ds(4608 + f * 64 + pos, 32, stride=2), :] = xf[
                            pl.ds((r * 2 + c) * 768 + f * 4 + pos * 2 + hq, 32, stride=24), :
                        ]
                out[:, pl.ds(head * LANES, LANES)] = xf[pl.ds(4608, 320)].astype(BF16)


def block(frames, stream, length, lens, cw, lw4, ew, gain, w):
    hbm = pl.BlockSpec(memory_space=pl.ANY)
    vmem = pl.BlockSpec(memory_space=pltpu.VMEM)
    smem = pl.BlockSpec(memory_space=pltpu.SMEM)
    dma = pltpu.SemaphoreType.DMA
    return pl.pallas_call(
        block_kernel,
        out_shape=(
            jax.ShapeDtypeStruct((5, 256, 512), BF16),
            jax.ShapeDtypeStruct((320, 1536), BF16),
        ),
        in_specs=[hbm, hbm, smem, vmem, hbm, vmem, vmem, vmem, vmem],
        out_specs=(hbm, vmem),
        scratch_shapes=[
            pltpu.VMEM((7, 256, 512), BF16),
            pltpu.VMEM((7, 18, 16, 1536), BF16),
            pltpu.VMEM((4, 1536, 512), BF16),
            pltpu.VMEM((768, 512), F32),
            pltpu.VMEM((5, 256, 512), BF16),
            pltpu.VMEM((5, 64, 3072), BF16),
            pltpu.VMEM((1536, LANES), F32),
            pltpu.VMEM((5, 32, 48, LANES), BF16),
            pltpu.VMEM((5, 32, 48, LANES), BF16),
            pltpu.VMEM((3, 2, 2, 4, 4, 96, 384), BF16),
            pltpu.VMEM((NCTX, 5, 48, LANES), BF16),
            pltpu.VMEM((NCTX, 5, 48, LANES), BF16),
            pltpu.VMEM((2, 8, LANES), jnp.int32),
            pltpu.VMEM((7680, LANES), F32),
            pltpu.VMEM((2, 320, 3072), BF16),
            pltpu.VMEM((320, 384), BF16),
            pltpu.VMEM((1536, LANES), F32),
            pltpu.VMEM((3, 2, NCTX, 24, LANES), BF16),
            pltpu.VMEM((3, 2, NCTX, 24, LANES), BF16),
            pltpu.VMEM((3, 2, NCTX, 24, LANES), BF16),
            dma((4,)), dma((2,)), dma((108,)), dma((108,)), dma, dma, dma((2,)), dma((2,)), dma((2,)), dma((8,)),
            dma((2,)), dma((2,)), dma((6,)), dma((6,)), dma((3,)),
        ],
        compiler_params=pltpu.CompilerParams(
            collective_id=0, has_side_effects=True, vmem_limit_bytes=63 * 2**20
        ),
        name="block",
    )(frames, stream, length, lens, cw, lw4, ew, gain, w)


def on_device(frames, stream, video_frames, conv_weight, latent_weight, embed_weight, norm_gain, qkv_weight):
    section, mixed = block(
        frames.reshape(5, 256, 512),
        stream.reshape(5, 64, 3072),
        video_frames,
        jnp.broadcast_to(video_frames[0], (8, LANES)),
        conv_weight.reshape(9, 1536, 512),
        jnp.tile(latent_weight, (1, 4)),
        embed_weight,
        norm_gain.reshape(1, 3072),
        qkv_weight,
    )
    return section.reshape(frames.shape), mixed.reshape(1, 5, 64, 1536)


def solution(mesh):
    finer = Mesh(mesh.devices.reshape(2, 2, 2, 4, 4), AXES)
    dp = ("xl", "co")
    return jax.shard_map(
        on_device,
        mesh=finer,
        in_specs=(
            P(dp, CTX, None, None, None),
            P(dp, CTX, None, None),
            P(dp),
            P(),
            P(),
            P(),
            P(),
            P(CTX, dp),
        ),
        out_specs=(P(dp, CTX, None, None, None), P(dp, CTX, None, None)),
        check_vma=False,
    )
```

```python
import jax
import jax.numpy as jnp
from jax import lax
from jax.experimental import pallas as pl
from jax.experimental.pallas import tpu as pltpu
from jax.sharding import Mesh
from jax.sharding import PartitionSpec as P

AXES = ("xl", "co", "xh", "y", "z")
CTX = ("xh", "y", "z")
MESH = pl.DeviceIdType.MESH
F32 = jnp.float32
BF16 = jnp.bfloat16
NCTX = 32
LANES = 128


def place():
    return {a: lax.axis_index(a) for a in AXES}


def ctx_of(me):
    return (me["xh"] * 4 + me["y"]) * 4 + me["z"]


def at_ctx(me, c, co=None):
    return (me["xl"], me["co"] if co is None else co, c // 16, (c // 4) % 4, c % 4)


def coordinate(me, axis):
    return (me["xh"] * 2 + me["xl"], me["y"], me["z"])[axis]


def moved(me, axis, c):
    if axis == 0:
        return (c % 2, me["co"], c // 2, me["y"], me["z"])
    if axis == 1:
        return (me["xl"], me["co"], me["xh"], c, me["z"])
    return (me["xl"], me["co"], me["xh"], me["y"], c)


def gather_copies(me, wall, ssem, rsem, r):
    rows = wall.shape[5] // 3
    stages = [[] for _ in range(6)]
    for part in range(3):
        for phase in range(3):
            axis = (part + phase) % 3
            full = [(part + i) % 3 for i in range(phase)]
            c = coordinate(me, axis)
            for step in range(2):
                for way in range(2):
                    sign = 1 - 2 * way
                    to = (c + sign + 4) % 4
                    held = c if step == 0 else (c - sign + 4) % 4
                    cut = rows // 2
                    begin = part * rows + (cut if step and way else 0)
                    size = rows if not step else rows - cut if way else cut
                    index = [r]
                    for a in range(3):
                        if a in full:
                            got = None
                        elif a == axis:
                            got = held
                        else:
                            got = coordinate(me, a)
                        if a == 0:
                            if got is None:
                                index += [pl.ds(0, 2), pl.ds(0, 2)]
                            else:
                                index += [got % 2, got // 2]
                        else:
                            index.append(pl.ds(0, 4) if got is None else got)
                    block = wall.at[(*index, pl.ds(begin, size))]
                    n = (((r * 3 + part) * 3 + phase) * 2 + step) * 2 + way
                    stages[phase * 2 + step].append(
                        pltpu.make_async_remote_copy(
                            src_ref=block,
                            dst_ref=block,
                            send_sem=ssem.at[n],
                            recv_sem=rsem.at[n],
                            device_id=moved(me, axis, to),
                            device_id_type=MESH,
                        )
                    )
    return stages


TICKS = (
    ((0, 0), (1, 0), (2, 0)),
    ((0, 1), (1, 1), (2, 1)),
    ((0, 2), (1, 2), (2, 2)),
    ((0, 3), (1, 3), (2, 3)),
    ((0, 4), (1, 4)),
    ((0, 5), (1, 5), (2, 4)),
    ((2, 5),),
)


def block_kernel(
    frames, stream, length, cw, lw, ew, gain, w,
    sec_out, out,
    xin, xcat, cwv, acc, secb, strm, nt, sb, sent, wall, xr, xs, lboth, xf, xm, qs, of, osd, osent, orr,
    cw_sem, in_sem, w_ssem, w_rsem, h_ssem, h_rsem, a_ssem, a_rsem, out_sem, own_sem,
    x_ssem, x_rsem, o_ssem, o_rsem, o_own,
):
    me = place()
    ctx = ctx_of(me)
    co = me["co"]
    lboth[0] = jnp.full((8, LANES), length[0], jnp.int32)
    place_w = [
        pltpu.make_async_copy(
            w.at[:, pl.ds(384 * r, 384)],
            wall.at[r, me["xl"], me["xh"], me["y"], me["z"]],
            own_sem.at[5 + r],
        )
        for r in range(3)
    ]
    for copy in place_w:
        copy.start()
    load_frames = pltpu.make_async_copy(frames, xin.at[pl.ds(2, 5)], in_sem.at[0])
    load_frames.start()

    def order(n):
        k = n % 9
        return (2 - k // 3) * 3 + k % 3

    def load_cw(n):
        return pltpu.make_async_copy(cw.at[order(n)], cwv.at[n % 4], cw_sem.at[n % 4])

    for n in range(3):
        load_cw(n).start()
    load_stream = pltpu.make_async_copy(stream, strm, in_sem.at[1])
    load_stream.start()

    barrier = pltpu.get_barrier_semaphore()

    @pl.loop(1, NCTX)
    def _(k):
        pl.semaphore_signal(
            barrier, inc=1, device_id=at_ctx(me, (ctx + k) % NCTX), device_id_type=MESH
        )

    @pl.loop(0, NCTX)
    def _(k):
        pl.semaphore_signal(
            barrier, inc=1, device_id=at_ctx(me, (ctx + k) % NCTX, 1 - co), device_id_type=MESH
        )

    x = coordinate(me, 0)
    for d in (1, 3):
        pl.semaphore_signal(
            barrier, inc=1, device_id=moved(me, 0, (x + d) % 4), device_id_type=MESH
        )
    pl.semaphore_wait(barrier, 2 * NCTX + 1)

    halo = pltpu.make_async_remote_copy(
        src_ref=frames.at[pl.ds(3, 2)],
        dst_ref=xin.at[pl.ds(0, 2)],
        send_sem=h_ssem,
        recv_sem=h_rsem,
        device_id=at_ctx(me, (ctx + 1) % NCTX),
        device_id_type=MESH,
    )
    halo.start()

    def swap(n, a, b):
        return pltpu.make_async_remote_copy(
            src_ref=a,
            dst_ref=b,
            send_sem=x_ssem.at[n],
            recv_sem=x_rsem.at[n],
            device_id=at_ctx(me, ctx, 1 - co),
            device_id_type=MESH,
        )

    swap_lens = swap(2, lboth.at[0], lboth.at[1])
    swap_lens.start()
    for copy in place_w:
        copy.wait()
    rounds = [gather_copies(me, wall, w_ssem, w_rsem, r) for r in range(3)]

    def tick(n):
        for r, stage in TICKS[n]:
            if stage:
                for copy in rounds[r][stage - 1]:
                    copy.wait_recv()
            for copy in rounds[r][stage]:
                copy.start()

    tick(0)

    edge = jnp.zeros((7, 1, 16, 1536), BF16)
    xcat[:, pl.ds(0, 1)] = edge
    xcat[:, pl.ds(17, 1)] = edge
    column = lax.broadcasted_iota(jnp.int32, (256, 512), 0) & 15

    def spread(i, factor):
        v = xin[i].astype(F32)
        act = (v / (1.0 + jnp.exp(-v))).astype(BF16).astype(F32) * factor
        before = jnp.where(column == 0, 0.0, pltpu.roll(act, 1, 0))
        after = jnp.where(column == 15, 0.0, pltpu.roll(act, 255, 0))
        for b, part in enumerate((before, act, after)):
            xcat[i, pl.ds(1, 16), :, pl.ds(512 * b, 512)] = part.astype(BF16).reshape(16, 16, 512)

    load_frames.wait()

    @pl.loop(2, 7)
    def _(i):
        spread(i, 1.0)

    tick(1)
    cell = lax.broadcasted_iota(jnp.int32, (256, 64), 0)
    lane = lax.broadcasted_iota(jnp.int32, (256, 64), 1)
    corner = ((cell >> 4) & 1) * 2 + (cell & 1)
    keep = jnp.where((lane >> 4) == corner, 1.0, 0.0)
    tok = lax.broadcasted_iota(jnp.int32, (64, 256), 0)
    cel = lax.broadcasted_iota(jnp.int32, (64, 256), 1)
    pick = jnp.where((cel >> 5) * 8 + ((cel & 15) >> 1) == tok, 1.0, 0.0).astype(BF16)
    source = lax.broadcasted_iota(jnp.int32, (16, 64), 0)
    target = lax.broadcasted_iota(jnp.int32, (16, 64), 1)
    copies = jnp.where((target & 15) == source, 1.0, 0.0).astype(BF16)
    count = length[0]

    def conv(first, many, checkpoints, begin):
        acc[pl.ds(0, many * 256)] = jnp.zeros((many * 256, 512), F32)

        @pl.loop(0, 9)
        def _(k):
            n = begin + k
            load_cw(n).wait()

            @pl.when(n < 15)
            def _():
                load_cw(n + 3).start()

            for when, now in checkpoints:
                @pl.when(k == when)
                def _():
                    tick(now)

            @pl.when(k == 6)
            def _():
                for f in range(many):
                    video = jnp.where(ctx * 5 + first + f < count, 1.0, 0.0)
                    acc[pl.ds(f * 256, 256)] = acc[pl.ds(f * 256, 256)] * video

            lag = 2 - k // 3
            slab = xcat[pl.ds(first + 2 - lag, many), pl.ds(k % 3, 16)]
            acc[pl.ds(0, many * 256)] += jnp.dot(
                slab.reshape(many * 256, 1536), cwv[n % 4], preferred_element_type=F32
            )

    def finish(first, many, n):
        @pl.loop(0, many)
        def _(i):
            t = first + i
            sec = (xin[t + 2].astype(F32) + acc[pl.ds(pl.multiple_of(i * 256, 256), 256)]).astype(BF16)
            secb[t] = sec
            lat = lax.dot_general(
                sec, lw[...], (((1,), (1,)), ((), ())), preferred_element_type=F32
            ).astype(BF16)
            lat = jnp.dot(lat, copies, preferred_element_type=F32)
            patches = jnp.dot(pick, (lat * keep).astype(BF16), preferred_element_type=F32).astype(BF16)
            e = jnp.dot(patches, ew[...], preferred_element_type=F32) + strm[t].astype(F32)
            scale = lax.rsqrt(jnp.mean(e * e, axis=-1, keepdims=True) + 1e-06)
            e = e * scale * gain[...]
            for j in range(24):
                nt[pl.ds(j, 64, stride=24), :] = e[:, j * LANES : (j + 1) * LANES]
            sb[t] = nt[...].astype(BF16).reshape(32, 48, LANES)

        span = pl.ds(first, many)
        pltpu.make_async_copy(secb.at[span], sec_out.at[span], out_sem.at[n]).start()
        stage = pltpu.make_async_copy(sb.at[span], sent.at[span], own_sem.at[1 + n])
        stage.start()
        stage.wait()

        @pl.loop(1, NCTX)
        def _(k):
            to = (ctx + k) % NCTX
            pltpu.make_async_remote_copy(
                src_ref=sent.at[span, to],
                dst_ref=xr.at[ctx, span],
                send_sem=a_ssem.at[n],
                recv_sem=a_rsem.at[n],
                device_id=at_ctx(me, to),
                device_id_type=MESH,
            ).start()

        pltpu.make_async_copy(sent.at[span, ctx], xr.at[ctx, span], own_sem.at[3 + n]).start()

    conv(2, 3, ((1, 2), (5, 3), (8, 4)), 0)
    load_stream.wait()
    finish(2, 3, 0)
    halo.wait_recv()
    inner = jnp.where(ctx > 0, 1.0, 0.0)

    @pl.loop(0, 2)
    def _(i):
        spread(i, inner)

    conv(0, 2, (), 9)
    finish(0, 2, 1)
    tick(5)
    swaps = []
    for n, (first, many) in enumerate(((2, 3), (0, 2))):
        span = pl.ds(first, many)
        bulk = xr.at[pl.ds(0, NCTX - 1), span]
        pltpu.make_async_copy(bulk, bulk, a_rsem.at[n]).wait()
        pltpu.make_async_copy(sent.at[span, ctx], xr.at[ctx, span], own_sem.at[3 + n]).wait()
        swaps.append(swap(n, xr.at[:, span], xs.at[:, span]))
        swaps[-1].start()

    def fill(g, src):
        xf[...] = src[...].astype(F32).reshape(7680, LANES)
        for f in range(5):
            for pos in range(2):
                for j in range(24):
                    xm[g, pl.ds(pos * 160 + f * 32, 32), pl.ds(j * LANES, LANES)] = xf[
                        pl.ds((f * 2 + pos) * 24 + j, 32, stride=240), :
                    ].astype(BF16)

    fill(0, xr)
    for copy in rounds[0][5]:
        copy.wait_recv()

    row = lax.broadcasted_iota(jnp.int32, (160, 160), 0)
    col = lax.broadcasted_iota(jnp.int32, (160, 160), 1)
    row_frame = (row & 31) * 5 + (row >> 5)
    col_frame = (col & 31) * 5 + (col >> 5)
    same = row == col

    def returned(r, g, to):
        return pltpu.make_async_remote_copy(
            src_ref=osent.at[r, g, to],
            dst_ref=orr.at[r, co, ctx],
            send_sem=o_ssem.at[r * 2 + g],
            recv_sem=o_rsem.at[r * 2 + g],
            device_id=at_ctx(me, to, co if g == 0 else 1 - co),
            device_id_type=MESH,
        )

    def kept(r):
        return pltpu.make_async_copy(osent.at[r, 0, ctx], orr.at[r, co, ctx], o_own.at[r])

    @pl.loop(0, 3)
    def _(r):
        @pl.when(r == 1)
        def _():
            tick(6)
            for copy in rounds[1][5]:
                copy.wait_recv()

        @pl.when(r == 2)
        def _():
            for copy in rounds[2][5]:
                copy.wait_recv()

        @pl.loop(0, 4)
        def _(q):
            @pl.when(r * 4 + q == 2)
            def _():
                swap_lens.wait_recv()
                for copy in swaps:
                    copy.wait_recv()
                fill(1, xs)

            g = q // 2
            hq = q % 2
            qs[...] = jnp.dot(
                xm[g], wall[r, hq].reshape(3072, 384), preferred_element_type=F32
            ).astype(BF16)
            most = jnp.broadcast_to(lboth[g, 0:1, 0:1], (160, 160))
            allowed = ((row_frame < most) & (col_frame < most)) | same
            for pos in range(2):
                rows = pl.ds(pos * 160, 160)
                scores = lax.dot_general(
                    qs[rows, 0:128], qs[rows, 128:256], (((1,), (1,)), ((), ())),
                    preferred_element_type=F32,
                ) * (128.0 ** -0.5)
                scores = jnp.where(allowed, scores, -1e30)
                expo = jnp.exp(scores - jnp.max(scores, axis=-1, keepdims=True))
                probs = (expo / jnp.sum(expo, axis=-1, keepdims=True)).astype(BF16)
                o = jnp.dot(probs, qs[rows, 256:384], preferred_element_type=F32)
                for f in range(5):
                    of[pl.ds(g * 768 + f * 4 + pos * 2 + hq, 32, stride=24), :] = o[
                        f * 32 : (f + 1) * 32
                    ]

        osd[r] = of[...].astype(BF16).reshape(2, NCTX, 24, LANES)
        stage = pltpu.make_async_copy(osd.at[r], osent.at[r], own_sem.at[0])
        stage.start()
        stage.wait()

        @pl.loop(1, NCTX)
        def _(k):
            returned(r, 0, (ctx + k) % NCTX).start()

        @pl.loop(0, NCTX)
        def _(k):
            returned(r, 1, (ctx + k) % NCTX).start()

        kept(r).start()

    for stages in rounds:
        for stage in stages:
            for copy in stage:
                copy.wait_send()
    halo.wait_send()
    swap_lens.wait_send()
    for copy in swaps:
        copy.wait_send()
    for n, (first, many) in enumerate(((2, 3), (0, 2))):
        span = pl.ds(first, many)
        bulk = xr.at[pl.ds(0, NCTX - 1), span]
        pltpu.make_async_copy(bulk, bulk, a_ssem.at[n]).wait()
        pltpu.make_async_copy(secb.at[span], sec_out.at[span], out_sem.at[n]).wait()
    for r in range(3):
        kept(r).wait()
        for g in range(2):
            bulk = orr.at[0, 0, pl.ds(0, NCTX - 1 + g)]
            pltpu.make_async_copy(bulk, bulk, o_rsem.at[r * 2 + g]).wait()
        xf[pl.ds(0, 1536)] = orr[r].astype(F32).reshape(1536, LANES)
        for c in range(2):
            for hq in range(2):
                head = 6 * hq + 3 * c + r
                base = 1536 + 320 * (r * 4 + c * 2 + hq)
                for f in range(5):
                    for pos in range(2):
                        xf[pl.ds(base + f * 64 + pos, 32, stride=2), :] = xf[
                            pl.ds(c * 768 + f * 4 + pos * 2 + hq, 32, stride=24), :
                        ]
                out[:, pl.ds(head * LANES, LANES)] = xf[pl.ds(base, 320)].astype(BF16)
    for r in range(3):
        for g in range(2):
            bulk = orr.at[0, 0, pl.ds(0, NCTX - 1 + g)]
            pltpu.make_async_copy(bulk, bulk, o_ssem.at[r * 2 + g]).wait()


def block(frames, stream, length, cw, lw, ew, gain, w):
    hbm = pl.BlockSpec(memory_space=pl.ANY)
    vmem = pl.BlockSpec(memory_space=pltpu.VMEM)
    smem = pl.BlockSpec(memory_space=pltpu.SMEM)
    dma = pltpu.SemaphoreType.DMA
    return pl.pallas_call(
        block_kernel,
        out_shape=(
            jax.ShapeDtypeStruct((5, 256, 512), BF16),
            jax.ShapeDtypeStruct((320, 1536), BF16),
        ),
        in_specs=[hbm, hbm, smem, hbm, vmem, vmem, vmem, vmem],
        out_specs=(hbm, vmem),
        scratch_shapes=[
            pltpu.VMEM((7, 256, 512), BF16),
            pltpu.VMEM((7, 18, 16, 1536), BF16),
            pltpu.VMEM((4, 1536, 512), BF16),
            pltpu.VMEM((768, 512), F32),
            pltpu.VMEM((5, 256, 512), BF16),
            pltpu.VMEM((5, 64, 3072), BF16),
            pltpu.VMEM((1536, LANES), F32),
            pltpu.VMEM((5, 32, 48, LANES), BF16),
            pltpu.VMEM((5, 32, 48, LANES), BF16),
            pltpu.VMEM((3, 2, 2, 4, 4, 96, 384), BF16),
            pltpu.VMEM((NCTX, 5, 48, LANES), BF16),
            pltpu.VMEM((NCTX, 5, 48, LANES), BF16),
            pltpu.VMEM((2, 8, LANES), jnp.int32),
            pltpu.VMEM((7680, LANES), F32),
            pltpu.VMEM((2, 320, 3072), BF16),
            pltpu.VMEM((320, 384), BF16),
            pltpu.VMEM((1536, LANES), F32),
            pltpu.VMEM((3, 2, NCTX, 24, LANES), BF16),
            pltpu.VMEM((3, 2, NCTX, 24, LANES), BF16),
            pltpu.VMEM((3, 2, NCTX, 24, LANES), BF16),
            dma((4,)), dma((2,)), dma((108,)), dma((108,)), dma, dma, dma((2,)), dma((2,)), dma((2,)), dma((8,)),
            dma((3,)), dma((3,)), dma((6,)), dma((6,)), dma((3,)),
        ],
        compiler_params=pltpu.CompilerParams(
            collective_id=0, has_side_effects=True, vmem_limit_bytes=63 * 2**20
        ),
        name="block",
    )(frames, stream, length, cw, lw, ew, gain, w)


def on_device(frames, stream, video_frames, conv_weight, latent_weight, embed_weight, norm_gain, qkv_weight):
    section, mixed = block(
        frames.reshape(5, 256, 512),
        stream.reshape(5, 64, 3072),
        video_frames,
        conv_weight.reshape(9, 1536, 512),
        latent_weight.T,
        embed_weight,
        norm_gain.reshape(1, 3072),
        qkv_weight,
    )
    return section.reshape(frames.shape), mixed.reshape(1, 5, 64, 1536)


def solution(mesh):
    finer = Mesh(mesh.devices.reshape(2, 2, 2, 4, 4), AXES)
    dp = ("xl", "co")
    return jax.shard_map(
        on_device,
        mesh=finer,
        in_specs=(
            P(dp, CTX, None, None, None),
            P(dp, CTX, None, None),
            P(dp),
            P(),
            P(),
            P(),
            P(),
            P(CTX, dp),
        ),
        out_specs=(P(dp, CTX, None, None, None), P(dp, CTX, None, None)),
        check_vma=False,
    )
```

```python
import jax
import jax.numpy as jnp
from jax import lax
from jax.experimental import pallas as pl
from jax.experimental.pallas import tpu as pltpu
from jax.sharding import Mesh
from jax.sharding import PartitionSpec as P

AXES = ("xl", "co", "xh", "y", "z")
CTX = ("xh", "y", "z")
MESH = pl.DeviceIdType.MESH
F32 = jnp.float32
BF16 = jnp.bfloat16
NCTX = 32
LANES = 128


def place():
    return {a: lax.axis_index(a) for a in AXES}


def ctx_of(me):
    return (me["xh"] * 4 + me["y"]) * 4 + me["z"]


def at_ctx(me, c, co=None):
    return (me["xl"], me["co"] if co is None else co, c // 16, (c // 4) % 4, c % 4)


def coordinate(me, axis):
    return (me["xh"] * 2 + me["xl"], me["y"], me["z"])[axis]


def moved(me, axis, c):
    if axis == 0:
        return (c % 2, me["co"], c // 2, me["y"], me["z"])
    if axis == 1:
        return (me["xl"], me["co"], me["xh"], c, me["z"])
    return (me["xl"], me["co"], me["xh"], me["y"], c)


def gather_copies(me, wall, ssem, rsem, r):
    rows = wall.shape[5] // 3
    stages = [[] for _ in range(6)]
    for part in range(3):
        for phase in range(3):
            axis = (part + phase) % 3
            full = [(part + i) % 3 for i in range(phase)]
            c = coordinate(me, axis)
            for step in range(2):
                for way in range(2):
                    sign = 1 - 2 * way
                    to = (c + sign + 4) % 4
                    held = c if step == 0 else (c - sign + 4) % 4
                    cut = rows // 2
                    begin = part * rows + (cut if step and way else 0)
                    size = rows if not step else rows - cut if way else cut
                    index = [r]
                    for a in range(3):
                        if a in full:
                            got = None
                        elif a == axis:
                            got = held
                        else:
                            got = coordinate(me, a)
                        if a == 0:
                            if got is None:
                                index += [pl.ds(0, 2), pl.ds(0, 2)]
                            else:
                                index += [got % 2, got // 2]
                        else:
                            index.append(pl.ds(0, 4) if got is None else got)
                    block = wall.at[(*index, pl.ds(begin, size))]
                    n = (((r * 3 + part) * 3 + phase) * 2 + step) * 2 + way
                    stages[phase * 2 + step].append(
                        pltpu.make_async_remote_copy(
                            src_ref=block,
                            dst_ref=block,
                            send_sem=ssem.at[n],
                            recv_sem=rsem.at[n],
                            device_id=moved(me, axis, to),
                            device_id_type=MESH,
                        )
                    )
    return stages


TICKS = (
    ((0, 0), (1, 0), (2, 0)),
    ((0, 1), (1, 1), (2, 1)),
    ((0, 2), (1, 2), (2, 2)),
    ((0, 3), (1, 3), (2, 3)),
    ((0, 4), (1, 4)),
    ((0, 5), (1, 5), (2, 4)),
    ((2, 5),),
)


def block_kernel(
    frames, stream, length, cw, lw, ew, gain, w,
    sec_out, out,
    xin, xcat, cwv, acc, secb, strm, nt, sb, sent, wall, xr, xs, lboth, xf, xm, qs, of, osd, osent, orr,
    cw_sem, in_sem, w_ssem, w_rsem, h_ssem, h_rsem, a_ssem, a_rsem, out_sem, own_sem,
    x_ssem, x_rsem, o_ssem, o_rsem, o_own,
):
    me = place()
    ctx = ctx_of(me)
    co = me["co"]
    lboth[0] = jnp.full((8, LANES), length[0], jnp.int32)
    place_w = [
        pltpu.make_async_copy(
            w.at[:, pl.ds(384 * r, 384)],
            wall.at[r, me["xl"], me["xh"], me["y"], me["z"]],
            own_sem.at[5 + r],
        )
        for r in range(3)
    ]
    for copy in place_w:
        copy.start()
    load_frames = pltpu.make_async_copy(frames, xin.at[pl.ds(2, 5)], in_sem.at[0])
    load_frames.start()

    def order(n):
        k = n % 9
        return (2 - k // 3) * 3 + k % 3

    def load_cw(n):
        return pltpu.make_async_copy(cw.at[order(n)], cwv.at[n % 4], cw_sem.at[n % 4])

    for n in range(3):
        load_cw(n).start()
    load_stream = pltpu.make_async_copy(stream, strm, in_sem.at[1])
    load_stream.start()

    barrier = pltpu.get_barrier_semaphore()

    @pl.loop(1, NCTX)
    def _(k):
        pl.semaphore_signal(
            barrier, inc=1, device_id=at_ctx(me, (ctx + k) % NCTX), device_id_type=MESH
        )

    @pl.loop(0, NCTX)
    def _(k):
        pl.semaphore_signal(
            barrier, inc=1, device_id=at_ctx(me, (ctx + k) % NCTX, 1 - co), device_id_type=MESH
        )

    x = coordinate(me, 0)
    for d in (1, 3):
        pl.semaphore_signal(
            barrier, inc=1, device_id=moved(me, 0, (x + d) % 4), device_id_type=MESH
        )
    pl.semaphore_wait(barrier, 2 * NCTX + 1)

    halo = pltpu.make_async_remote_copy(
        src_ref=frames.at[pl.ds(3, 2)],
        dst_ref=xin.at[pl.ds(0, 2)],
        send_sem=h_ssem,
        recv_sem=h_rsem,
        device_id=at_ctx(me, (ctx + 1) % NCTX),
        device_id_type=MESH,
    )
    halo.start()

    def swap(n, a, b):
        return pltpu.make_async_remote_copy(
            src_ref=a,
            dst_ref=b,
            send_sem=x_ssem.at[n],
            recv_sem=x_rsem.at[n],
            device_id=at_ctx(me, ctx, 1 - co),
            device_id_type=MESH,
        )

    swap_lens = swap(2, lboth.at[0], lboth.at[1])
    swap_lens.start()
    for copy in place_w:
        copy.wait()
    rounds = [gather_copies(me, wall, w_ssem, w_rsem, r) for r in range(3)]

    def tick(n):
        for r, stage in TICKS[n]:
            phase = stage // 2
            for axis in range(3):
                part = (axis - phase) % 3
                both = slice(2 * part, 2 * part + 2)
                if stage:
                    for copy in rounds[r][stage - 1][both]:
                        copy.wait_recv()
                for copy in rounds[r][stage][both]:
                    copy.start()

    tick(0)

    edge = jnp.zeros((7, 1, 16, 1536), BF16)
    xcat[:, pl.ds(0, 1)] = edge
    xcat[:, pl.ds(17, 1)] = edge
    column = lax.broadcasted_iota(jnp.int32, (256, 512), 0) & 15

    def spread(i, factor):
        v = xin[i].astype(F32)
        act = (v / (1.0 + jnp.exp(-v))).astype(BF16).astype(F32) * factor
        before = jnp.where(column == 0, 0.0, pltpu.roll(act, 1, 0))
        after = jnp.where(column == 15, 0.0, pltpu.roll(act, 255, 0))
        for b, part in enumerate((before, act, after)):
            xcat[i, pl.ds(1, 16), :, pl.ds(512 * b, 512)] = part.astype(BF16).reshape(16, 16, 512)

    load_frames.wait()

    @pl.loop(2, 7)
    def _(i):
        spread(i, 1.0)

    tick(1)
    cell = lax.broadcasted_iota(jnp.int32, (256, 64), 0)
    lane = lax.broadcasted_iota(jnp.int32, (256, 64), 1)
    corner = ((cell >> 4) & 1) * 2 + (cell & 1)
    keep = jnp.where((lane >> 4) == corner, 1.0, 0.0)
    tok = lax.broadcasted_iota(jnp.int32, (64, 256), 0)
    cel = lax.broadcasted_iota(jnp.int32, (64, 256), 1)
    pick = jnp.where((cel >> 5) * 8 + ((cel & 15) >> 1) == tok, 1.0, 0.0).astype(BF16)
    source = lax.broadcasted_iota(jnp.int32, (16, 64), 0)
    target = lax.broadcasted_iota(jnp.int32, (16, 64), 1)
    copies = jnp.where((target & 15) == source, 1.0, 0.0).astype(BF16)
    count = length[0]

    def conv(first, many, checkpoints, begin):
        acc[pl.ds(0, many * 256)] = jnp.zeros((many * 256, 512), F32)

        @pl.loop(0, 9)
        def _(k):
            n = begin + k
            load_cw(n).wait()

            @pl.when(n < 15)
            def _():
                load_cw(n + 3).start()

            for when, now in checkpoints:
                @pl.when(k == when)
                def _():
                    tick(now)

            @pl.when(k == 6)
            def _():
                for f in range(many):
                    video = jnp.where(ctx * 5 + first + f < count, 1.0, 0.0)
                    acc[pl.ds(f * 256, 256)] = acc[pl.ds(f * 256, 256)] * video

            lag = 2 - k // 3
            slab = xcat[pl.ds(first + 2 - lag, many), pl.ds(k % 3, 16)]
            acc[pl.ds(0, many * 256)] += jnp.dot(
                slab.reshape(many * 256, 1536), cwv[n % 4], preferred_element_type=F32
            )

    def finish(first, many, n):
        @pl.loop(0, many)
        def _(i):
            t = first + i
            sec = (xin[t + 2].astype(F32) + acc[pl.ds(pl.multiple_of(i * 256, 256), 256)]).astype(BF16)
            secb[t] = sec
            lat = lax.dot_general(
                sec, lw[...], (((1,), (1,)), ((), ())), preferred_element_type=F32
            ).astype(BF16)
            lat = jnp.dot(lat, copies, preferred_element_type=F32)
            patches = jnp.dot(pick, (lat * keep).astype(BF16), preferred_element_type=F32).astype(BF16)
            e = jnp.dot(patches, ew[...], preferred_element_type=F32) + strm[t].astype(F32)
            scale = lax.rsqrt(jnp.mean(e * e, axis=-1, keepdims=True) + 1e-06)
            e = e * scale * gain[...]
            for j in range(24):
                nt[pl.ds(j, 64, stride=24), :] = e[:, j * LANES : (j + 1) * LANES]
            sb[t] = nt[...].astype(BF16).reshape(32, 48, LANES)

        span = pl.ds(first, many)
        pltpu.make_async_copy(secb.at[span], sec_out.at[span], out_sem.at[n]).start()
        stage = pltpu.make_async_copy(sb.at[span], sent.at[span], own_sem.at[1 + n])
        stage.start()
        stage.wait()

        @pl.loop(1, NCTX)
        def _(k):
            to = (ctx + k) % NCTX
            pltpu.make_async_remote_copy(
                src_ref=sent.at[span, to],
                dst_ref=xr.at[ctx, span],
                send_sem=a_ssem.at[n],
                recv_sem=a_rsem.at[n],
                device_id=at_ctx(me, to),
                device_id_type=MESH,
            ).start()

        pltpu.make_async_copy(sent.at[span, ctx], xr.at[ctx, span], own_sem.at[3 + n]).start()

    conv(2, 3, ((1, 2), (5, 3), (8, 4)), 0)
    load_stream.wait()
    finish(2, 3, 0)
    halo.wait_recv()
    inner = jnp.where(ctx > 0, 1.0, 0.0)

    @pl.loop(0, 2)
    def _(i):
        spread(i, inner)

    conv(0, 2, (), 9)
    finish(0, 2, 1)
    tick(5)
    swaps = []
    for n, (first, many) in enumerate(((2, 3), (0, 2))):
        span = pl.ds(first, many)
        bulk = xr.at[pl.ds(0, NCTX - 1), span]
        pltpu.make_async_copy(bulk, bulk, a_rsem.at[n]).wait()
        pltpu.make_async_copy(sent.at[span, ctx], xr.at[ctx, span], own_sem.at[3 + n]).wait()
        swaps.append(swap(n, xr.at[:, span], xs.at[:, span]))
        swaps[-1].start()

    def fill(g, src):
        xf[...] = src[...].astype(F32).reshape(7680, LANES)
        for f in range(5):
            for pos in range(2):
                for j in range(24):
                    xm[g, pl.ds(pos * 160 + f * 32, 32), pl.ds(j * LANES, LANES)] = xf[
                        pl.ds((f * 2 + pos) * 24 + j, 32, stride=240), :
                    ].astype(BF16)

    fill(0, xr)
    for copy in rounds[0][5]:
        copy.wait_recv()

    row = lax.broadcasted_iota(jnp.int32, (160, 160), 0)
    col = lax.broadcasted_iota(jnp.int32, (160, 160), 1)
    row_frame = (row & 31) * 5 + (row >> 5)
    col_frame = (col & 31) * 5 + (col >> 5)
    same = row == col

    def returned(r, g, to):
        return pltpu.make_async_remote_copy(
            src_ref=osent.at[r, g, to],
            dst_ref=orr.at[r, co, ctx],
            send_sem=o_ssem.at[r * 2 + g],
            recv_sem=o_rsem.at[r * 2 + g],
            device_id=at_ctx(me, to, co if g == 0 else 1 - co),
            device_id_type=MESH,
        )

    def kept(r):
        return pltpu.make_async_copy(osent.at[r, 0, ctx], orr.at[r, co, ctx], o_own.at[r])

    @pl.loop(0, 3)
    def _(r):
        @pl.when(r == 1)
        def _():
            for copy in rounds[1][5]:
                copy.wait_recv()

        @pl.when(r == 2)
        def _():
            for copy in rounds[2][5]:
                copy.wait_recv()

        @pl.loop(0, 4)
        def _(q):
            @pl.when(r * 4 + q == 6)
            def _():
                tick(6)

            @pl.when(r * 4 + q == 2)
            def _():
                swap_lens.wait_recv()
                for copy in swaps:
                    copy.wait_recv()
                fill(1, xs)

            g = q // 2
            hq = q % 2
            qs[...] = jnp.dot(
                xm[g], wall[r, hq].reshape(3072, 384), preferred_element_type=F32
            ).astype(BF16)
            most = jnp.broadcast_to(lboth[g, 0:1, 0:1], (160, 160))
            allowed = ((row_frame < most) & (col_frame < most)) | same
            for pos in range(2):
                rows = pl.ds(pos * 160, 160)
                scores = lax.dot_general(
                    qs[rows, 0:128], qs[rows, 128:256], (((1,), (1,)), ((), ())),
                    preferred_element_type=F32,
                ) * (128.0 ** -0.5)
                scores = jnp.where(allowed, scores, -1e30)
                expo = jnp.exp(scores - jnp.max(scores, axis=-1, keepdims=True))
                probs = (expo / jnp.sum(expo, axis=-1, keepdims=True)).astype(BF16)
                o = jnp.dot(probs, qs[rows, 256:384], preferred_element_type=F32)
                for f in range(5):
                    of[pl.ds(g * 768 + f * 4 + pos * 2 + hq, 32, stride=24), :] = o[
                        f * 32 : (f + 1) * 32
                    ]

        osd[r] = of[...].astype(BF16).reshape(2, NCTX, 24, LANES)
        stage = pltpu.make_async_copy(osd.at[r], osent.at[r], own_sem.at[0])
        stage.start()
        stage.wait()

        @pl.loop(1, NCTX)
        def _(k):
            returned(r, 0, (ctx + k) % NCTX).start()

        @pl.loop(0, NCTX)
        def _(k):
            returned(r, 1, (ctx + k) % NCTX).start()

        kept(r).start()

    for stages in rounds:
        for stage in stages:
            for copy in stage:
                copy.wait_send()
    halo.wait_send()
    swap_lens.wait_send()
    for copy in swaps:
        copy.wait_send()
    for n, (first, many) in enumerate(((2, 3), (0, 2))):
        span = pl.ds(first, many)
        bulk = xr.at[pl.ds(0, NCTX - 1), span]
        pltpu.make_async_copy(bulk, bulk, a_ssem.at[n]).wait()
        pltpu.make_async_copy(secb.at[span], sec_out.at[span], out_sem.at[n]).wait()
    for r in range(3):
        kept(r).wait()
        for g in range(2):
            bulk = orr.at[0, 0, pl.ds(0, NCTX - 1 + g)]
            pltpu.make_async_copy(bulk, bulk, o_rsem.at[r * 2 + g]).wait()
        xf[pl.ds(0, 1536)] = orr[r].astype(F32).reshape(1536, LANES)
        for c in range(2):
            for hq in range(2):
                head = 6 * hq + 3 * c + r
                base = 1536 + 320 * (r * 4 + c * 2 + hq)
                for f in range(5):
                    for pos in range(2):
                        xf[pl.ds(base + f * 64 + pos, 32, stride=2), :] = xf[
                            pl.ds(c * 768 + f * 4 + pos * 2 + hq, 32, stride=24), :
                        ]
                out[:, pl.ds(head * LANES, LANES)] = xf[pl.ds(base, 320)].astype(BF16)
    for r in range(3):
        for g in range(2):
            bulk = orr.at[0, 0, pl.ds(0, NCTX - 1 + g)]
            pltpu.make_async_copy(bulk, bulk, o_ssem.at[r * 2 + g]).wait()


def block(frames, stream, length, cw, lw, ew, gain, w):
    hbm = pl.BlockSpec(memory_space=pl.ANY)
    vmem = pl.BlockSpec(memory_space=pltpu.VMEM)
    smem = pl.BlockSpec(memory_space=pltpu.SMEM)
    dma = pltpu.SemaphoreType.DMA
    return pl.pallas_call(
        block_kernel,
        out_shape=(
            jax.ShapeDtypeStruct((5, 256, 512), BF16),
            jax.ShapeDtypeStruct((320, 1536), BF16),
        ),
        in_specs=[hbm, hbm, smem, hbm, vmem, vmem, vmem, vmem],
        out_specs=(hbm, vmem),
        scratch_shapes=[
            pltpu.VMEM((7, 256, 512), BF16),
            pltpu.VMEM((7, 18, 16, 1536), BF16),
            pltpu.VMEM((4, 1536, 512), BF16),
            pltpu.VMEM((768, 512), F32),
            pltpu.VMEM((5, 256, 512), BF16),
            pltpu.VMEM((5, 64, 3072), BF16),
            pltpu.VMEM((1536, LANES), F32),
            pltpu.VMEM((5, 32, 48, LANES), BF16),
            pltpu.VMEM((5, 32, 48, LANES), BF16),
            pltpu.VMEM((3, 2, 2, 4, 4, 96, 384), BF16),
            pltpu.VMEM((NCTX, 5, 48, LANES), BF16),
            pltpu.VMEM((NCTX, 5, 48, LANES), BF16),
            pltpu.VMEM((2, 8, LANES), jnp.int32),
            pltpu.VMEM((7680, LANES), F32),
            pltpu.VMEM((2, 320, 3072), BF16),
            pltpu.VMEM((320, 384), BF16),
            pltpu.VMEM((1536, LANES), F32),
            pltpu.VMEM((3, 2, NCTX, 24, LANES), BF16),
            pltpu.VMEM((3, 2, NCTX, 24, LANES), BF16),
            pltpu.VMEM((3, 2, NCTX, 24, LANES), BF16),
            dma((4,)), dma((2,)), dma((108,)), dma((108,)), dma, dma, dma((2,)), dma((2,)), dma((2,)), dma((8,)),
            dma((3,)), dma((3,)), dma((6,)), dma((6,)), dma((3,)),
        ],
        compiler_params=pltpu.CompilerParams(
            collective_id=0, has_side_effects=True, vmem_limit_bytes=63 * 2**20
        ),
        name="block",
    )(frames, stream, length, cw, lw, ew, gain, w)


def on_device(frames, stream, video_frames, conv_weight, latent_weight, embed_weight, norm_gain, qkv_weight):
    section, mixed = block(
        frames.reshape(5, 256, 512),
        stream.reshape(5, 64, 3072),
        video_frames,
        conv_weight.reshape(9, 1536, 512),
        latent_weight.T,
        embed_weight,
        norm_gain.reshape(1, 3072),
        qkv_weight,
    )
    return section.reshape(frames.shape), mixed.reshape(1, 5, 64, 1536)


def solution(mesh):
    finer = Mesh(mesh.devices.reshape(2, 2, 2, 4, 4), AXES)
    dp = ("xl", "co")
    return jax.shard_map(
        on_device,
        mesh=finer,
        in_specs=(
            P(dp, CTX, None, None, None),
            P(dp, CTX, None, None),
            P(dp),
            P(),
            P(),
            P(),
            P(),
            P(CTX, dp),
        ),
        out_specs=(P(dp, CTX, None, None, None), P(dp, CTX, None, None)),
        check_vma=False,
    )
```
